32 devices in a mesh: clip: 2 (over x), blk: 16 (over z, y, core).
Axes of the slice: x: 2, y: 2, z: 4, core: 2. Of those that a mesh axis runs over, the one named last changes fastest.
Arguments:
- queries: bfloat16 [8192, 2560], P(('clip', 'blk')), parts along dimension 0, may hold values from -24 to 24
- keys: bfloat16 [8192, 2560], P(('clip', 'blk')), parts along dimension 0, may hold values from -24 to 24
- values: bfloat16 [8192, 2560], P(('clip', 'blk')), parts along dimension 0, may hold values from -6 to 6
- kept_blocks: int32 [64, 8], P(('clip', 'blk')), parts along dimension 0, may hold values from 0 to 31, as said below
Outputs:
- attended: bfloat16 [8192, 2560], P(('clip', 'blk')), parts along dimension 0
The draws below stay inside these ranges and needn't reach their ends.
There are 2 independent parts, one for each index of `clip`. The reference program is written for one: setup_inputs(seed, part) draws one part's arguments, and reference() takes and returns one part's arrays. A program takes and returns all parts, laid end to end along the dimension named above; each array names one. Nothing has to cross between parts.
Inputs may be any that keep to these rules, and one draw needn't show every extreme that they name: `kept_blocks`: row b lists 8 distinct key blocks in increasing order; b itself is one of them, and for every listed block j the difference j // 2 - b // 2 is 0 or plus or minus a power of two of at most 8.
All inputs are finite; a program needn't handle non-finite values.
Results may differ from the reference program's by a relative error of at most 0.0065.
Values may be sent and summed in bfloat16 or wider, within the bound.
A program may use at most 128 MiB of HBM per device.

```python
import math
import jax
import jax.numpy as jnp
from jax import lax

H = 20
DH = 128
BLOCK = 128
BD = 2
KEEP = 8
REACH = 8
NB = 32
SEQ = 4096


def draw_queries(key, part):
    values_drawn = jnp.clip(jax.random.normal(jax.random.fold_in(key, 1), (SEQ, H * DH), jnp.float32), -4.0, 4.0)
    return values_drawn.astype(jnp.bfloat16)


def draw_keys(key, part):
    values_drawn = jnp.clip(jax.random.normal(jax.random.fold_in(key, 2), (SEQ, H * DH), jnp.float32), -4.0, 4.0)
    return values_drawn.astype(jnp.bfloat16)


def draw_kept_blocks(key, part):
    blocks = jnp.arange(NB, dtype=jnp.int32)
    owner_device = blocks // BD
    offsets = [0]
    distance = 1
    farthest = min(REACH, NB // BD - 1)
    while distance <= farthest:
        offsets = offsets + [distance, -distance]
        distance = distance * 2
    columns = []
    for offset in offsets:
        for within in range(BD):
            columns.append((owner_device + offset) * BD + within)
    candidates = jnp.stack(columns, axis=1).astype(jnp.int32)
    candidate_count = candidates.shape[1]
    usable = (candidates >= 0) & (candidates < NB) & (candidates != blocks[:, None])
    random_rank = jax.random.randint(jax.random.fold_in(key, 7), (NB, candidate_count), 0, 4096, dtype=jnp.int32)
    ranking = jnp.where(usable, random_rank * candidate_count + jnp.arange(candidate_count, dtype=jnp.int32)[None, :], -1)
    ranked, picked = lax.top_k(ranking, KEEP - 1)
    chosen = jnp.take_along_axis(candidates, picked, axis=1)
    return jnp.sort(jnp.concatenate([blocks[:, None], chosen], axis=1), axis=1).astype(jnp.int32)


def shard_levels(rng, extent, shards, low, largest):
    loudness = 1.0
    for dim, blocks in shards:
        steps = jax.random.uniform(jax.random.fold_in(jax.random.fold_in(rng, 6), dim), (blocks,), jnp.float32, low / len(shards), largest / len(shards))
        loudness = loudness * jnp.repeat(jnp.exp(steps), extent[dim] // blocks).reshape((-1,) + (1,) * (len(extent) - 1 - dim))
    return loudness


def scatter_about(rng, dims, spread, bound, shards=(), held_as=jnp.bfloat16):
    array = spread * jax.random.normal(rng, dims, jnp.float32)
    if shards:
        array = array * shard_levels(rng, dims, shards, -0.22, 0.18)
    return jnp.clip(array, -bound, bound).astype(held_as)


def setup_inputs(seed: int = 0, part: int = 0) -> dict:
    key_list = jax.random.split(jax.random.key(seed), 5)
    part_splits = jax.random.split(jax.random.fold_in(key_list[4], part), 5)
    queries = draw_queries(jax.random.fold_in(jax.random.fold_in(key_list[4], part), 71), part)
    keys = draw_keys(jax.random.fold_in(jax.random.fold_in(key_list[4], part), 71), part)
    values = scatter_about(part_splits[2], (SEQ, H * DH), 1.0, 6.0, ((0, 16),))
    kept_blocks = draw_kept_blocks(jax.random.fold_in(jax.random.fold_in(key_list[4], part), 71), part)
    return dict(queries=queries, keys=keys, values=values, kept_blocks=kept_blocks)


def reference(queries, keys, values, kept_blocks):
    query_all = queries.reshape(NB, BLOCK, H, DH)
    key_all = keys.reshape(NB, BLOCK, H, DH)
    value_all = values.reshape(NB, BLOCK, H, DH)
    scale_factor = 1.0 / math.sqrt(DH)

    def attend_block(block_number):
        listed = kept_blocks[block_number].astype(jnp.int32)
        query_rows = query_all[block_number].astype(jnp.float32)
        key_rows = key_all[listed].reshape(KEEP * BLOCK, H, DH).astype(jnp.float32)
        value_rows = value_all[listed].reshape(KEEP * BLOCK, H, DH).astype(jnp.float32)
        scores = jnp.einsum('qhd,khd->hqk', query_rows, key_rows) * scale_factor
        top = lax.optimization_barrier(jnp.max(scores, axis=-1))
        weight = jnp.exp(scores - top[..., None])
        total = lax.optimization_barrier(jnp.sum(weight, axis=-1))
        rounded = lax.optimization_barrier(weight.astype(jnp.bfloat16)).astype(jnp.float32)
        numerator = jnp.einsum('hqk,khd->qhd', rounded, value_rows)
        result = numerator / jnp.transpose(total)[:, :, None]
        return result.astype(jnp.bfloat16)
    outputs = lax.map(attend_block, jnp.arange(NB, dtype=jnp.int32))
    return outputs.reshape(SEQ, H * DH)
```

```python
import functools
import math

import jax
import jax.numpy as jnp
from jax import lax
from jax.experimental import pallas as pl
from jax.experimental.pallas import tpu as pltpu
from jax.sharding import PartitionSpec as P

DH = 128
BLOCK = 128
HEADS_PER_GROUP = 1
LEAD = 3

OFFSETS = (1, -1, 2, -2, 4, -4, 8, -8, 0)
OWN = 8
MASKED = -1e30
C_EXP = math.log2(math.e) / math.sqrt(DH)


def kernel(
    n, groups, kept_ref, q_hbm, k_hbm, v_hbm, out_ref,
    kv, q_vmem, scores, bias, local_sem, q_sem, send_sem, recv_sem,
):
    width = kv.shape[-1]
    rows = kv.shape[-2]
    local_blocks = rows // BLOCK
    d = lax.axis_index("blk")
    r = lax.rem(d, 4)
    upper = r // 2
    odd = lax.rem(r, 2)

    pair = d + 2 - 4 * upper
    mate = d + 1 - 2 * odd
    has_up = d + 4 < n
    has_down = d - 4 >= 0

    def columns(g):
        return pl.ds(pl.multiple_of(g * width, width), width)

    def local_copies(g):
        return [
            pltpu.make_async_copy(hbm.at[:, columns(g)], kv.at[OWN, g, i], local_sem.at[i, g])
            for i, hbm in ((0, k_hbm), (1, v_hbm))
        ]

    def flow(index, src_slot, dst_slot, target, g):
        return pltpu.make_async_remote_copy(
            src_ref=kv.at[src_slot, g],
            dst_ref=kv.at[dst_slot, g],
            send_sem=send_sem.at[index, g],
            recv_sem=recv_sem.at[dst_slot, g],
            device_id={"blk": target},
            device_id_type=pl.DeviceIdType.MESH,
        )

    def received(slot, sender, g):
        return pltpu.make_async_remote_copy(
            src_ref=kv.at[slot, g],
            dst_ref=kv.at[slot, g],
            send_sem=send_sem.at[0, g],
            recv_sem=recv_sem.at[slot, g],
            device_id={"blk": sender},
            device_id_type=pl.DeviceIdType.MESH,
        )

    own_flows = (
        (0, OWN, 5, d + 4, has_up),
        (1, OWN, 4, d - 4, has_down),
        (2, OWN, 3 - upper, pair, None),
        (3, OWN, 1 - odd, mate, None),
    )
    both = jnp.logical_and(has_up, has_down)
    pass_flows = (
        (4, 5, 7, d + 4, both),
        (5, 4, 6, d - 4, both),
        (6, 4 + upper, 2 + upper, pair, jnp.where(upper == 1, d - 4 >= 0, d + 4 < n)),
    )
    mate_flows = (
        (7, 2 + odd, odd, mate, jnp.where(odd == 1, d - 2 >= 0, d + 2 < n)),
    )

    def when(condition, action):
        if condition is None:
            action()
        else:
            pl.when(condition)(action)

    def start(flows, g):
        for index, src, dst, target, condition in flows:
            when(condition, lambda: flow(index, src, dst, target, g).start())

    def arrive(slot, sender, condition, g):
        when(condition, lambda: received(slot, sender, g).wait_recv())

    pl.loop(0, groups)(lambda g: [c.start() for c in local_copies(g)] and None)
    q_copy = pltpu.make_async_copy(q_hbm, q_vmem, q_sem)
    q_copy.start()

    barrier = pltpu.get_barrier_semaphore()
    for target, condition in ((d + 4, has_up), (d - 4, has_down), (pair, None), (mate, None)):
        when(
            condition,
            lambda: pl.semaphore_signal(
                barrier, inc=1, device_id={"blk": target}, device_id_type=pl.DeviceIdType.MESH
            ),
        )
    pl.semaphore_wait(barrier, 2 + has_up.astype(jnp.int32) + has_down.astype(jnp.int32))

    def send_own(g):
        for c in local_copies(g):
            c.wait()
        start(own_flows, g)

    for g in range(min(LEAD, groups)):
        send_own(g)

    for slot, offset in enumerate(OFFSETS[:OWN]):
        source = d + offset

        @pl.when(jnp.logical_or(source < 0, source >= n))
        def _():
            @pl.loop(0, groups)
            def _(g):
                kv[slot, g] = jnp.zeros(kv.shape[2:], kv.dtype)

    for query_slot in range(local_blocks):
        kept = [kept_ref[query_slot, j] for j in range(kept_ref.shape[1])]
        for slot, offset in enumerate(OFFSETS):
            for key_slot in range(local_blocks):
                block = (d + offset) * local_blocks + key_slot
                allowed = functools.reduce(jnp.logical_or, [j == block for j in kept])
                allowed = jnp.logical_and(allowed, jnp.logical_and(d + offset >= 0, d + offset < n))
                bias[pl.ds(query_slot, 1), pl.ds(slot * rows + key_slot * BLOCK, BLOCK)] = jnp.full(
                    (1, BLOCK), jnp.where(allowed, 0.0, MASKED), jnp.float32
                )
    q_copy.wait()

    def attend(g):
        for head in range(width // DH):
            lanes = pl.ds(head * DH, DH)
            q = q_vmem[:, pl.ds(pl.multiple_of(g * width + head * DH, DH), DH)]
            tops = [None] * local_blocks
            for slot in range(len(OFFSETS)):
                s = lax.dot_general(
                    q, kv[slot, g, 0, :, lanes], (((1,), (1,)), ((), ())),
                    preferred_element_type=jnp.float32,
                )
                for b in range(local_blocks):
                    part = s[b * BLOCK : (b + 1) * BLOCK] + bias[b : b + 1, slot * rows : (slot + 1) * rows]
                    scores[slot, b * BLOCK : (b + 1) * BLOCK] = part
                    tops[b] = part if tops[b] is None else jnp.maximum(tops[b], part)
            top = jnp.concatenate([jnp.max(t, axis=1, keepdims=True) for t in tops], axis=0)
            sums = None
            numerator = None
            for slot in range(len(OFFSETS)):
                weight = jnp.exp2((scores[slot] - top) * C_EXP)
                sums = weight if sums is None else sums + weight
                term = jnp.dot(
                    weight.astype(jnp.bfloat16), kv[slot, g, 1, :, lanes],
                    preferred_element_type=jnp.float32,
                )
                numerator = term if numerator is None else numerator + term
            total = jnp.sum(sums, axis=1, keepdims=True)
            out_ref[:, pl.ds(pl.multiple_of(g * width + head * DH, DH), DH)] = (
                numerator / total
            ).astype(out_ref.dtype)

    @pl.loop(0, groups + 2)
    def _(t):
        @pl.when(t + LEAD < groups)
        def _():
            send_own(t + LEAD)

        @pl.when(t < groups)
        def _():
            arrive(5, d - 4, has_down, t)
            arrive(4, d + 4, has_up, t)
            start(pass_flows, t)

        @pl.when(jnp.logical_and(t >= 1, t < groups + 1))
        def _():
            g = t - 1
            arrive(2 + upper, pair, None, g)
            arrive(3 - upper, pair, jnp.where(upper == 1, d + 2 < n, d - 2 >= 0), g)
            start(mate_flows, g)

        @pl.when(t >= 2)
        def _():
            g = t - 2
            arrive(odd, mate, None, g)
            arrive(1 - odd, mate, jnp.where(odd == 1, d + 1 < n, d - 1 >= 0), g)
            arrive(7, d - 4, d - 8 >= 0, g)
            arrive(6, d + 4, d + 8 < n, g)
            attend(g)

    @pl.loop(0, groups)
    def _(g):
        for index, src, dst, target, condition in own_flows + pass_flows + mate_flows:
            when(condition, lambda: flow(index, src, dst, target, g).wait_send())


def per_device(queries, keys, values, kept_blocks):
    n = lax.axis_size("blk")
    rows, features = queries.shape
    width = HEADS_PER_GROUP * DH
    groups = features // width
    slots = len(OFFSETS)
    return pl.pallas_call(
        functools.partial(kernel, n, groups),
        out_shape=jax.ShapeDtypeStruct((rows, features), jnp.bfloat16),
        in_specs=[pl.BlockSpec(memory_space=pltpu.SMEM)] + [pl.BlockSpec(memory_space=pl.ANY)] * 3,
        out_specs=pl.BlockSpec(memory_space=pltpu.VMEM),
        scratch_shapes=[
            pltpu.VMEM((slots, groups, 2, rows, width), jnp.bfloat16),
            pltpu.VMEM((rows, features), jnp.bfloat16),
            pltpu.VMEM((slots, rows, rows), jnp.float32),
            pltpu.VMEM((rows // BLOCK, slots * rows), jnp.float32),
            pltpu.SemaphoreType.DMA((2, groups)),
            pltpu.SemaphoreType.DMA,
            pltpu.SemaphoreType.DMA((8, groups)),
            pltpu.SemaphoreType.DMA((8, groups)),
        ],
        compiler_params=pltpu.CompilerParams(
            collective_id=0, has_side_effects=True, vmem_limit_bytes=48 * 2**20
        ),
    )(kept_blocks, queries, keys, values)


def solution(mesh):
    placed = P(("clip", "blk"), None)
    return jax.shard_map(
        per_device, mesh=mesh, in_specs=(placed,) * 4, out_specs=placed, check_vma=False
    )
```

```python
import functools
import math

import jax
import jax.numpy as jnp
from jax import lax
from jax.experimental import pallas as pl
from jax.experimental.pallas import tpu as pltpu
from jax.sharding import PartitionSpec as P

DH = 128
BLOCK = 128
HEADS_PER_GROUP = 1
LEAD = 1

OFFSETS = (1, -1, 2, -2, 4, -4, 8, -8, 0)
OWN = 8
MASKED = -1e30
C_EXP = math.log2(math.e) / math.sqrt(DH)


def kernel(
    n, groups, kept_hbm, q_hbm, k_hbm, v_hbm, out_hbm,
    kv, kept_ref, q_vmem, scores, bias, out_ref, local_sem, kept_sem, q_sem, out_sem, send_sem, recv_sem,
):
    width = kv.shape[-1]
    rows = kv.shape[-2]
    local_blocks = rows // BLOCK
    d = lax.axis_index("blk")
    r = lax.rem(d, 4)
    upper = r // 2
    odd = lax.rem(r, 2)

    pair = d + 2 - 4 * upper
    mate = d + 1 - 2 * odd
    has_up = d + 4 < n
    has_down = d - 4 >= 0

    def columns(g):
        return pl.ds(pl.multiple_of(g * width, width), width)

    def local_copies(g):
        return [
            pltpu.make_async_copy(hbm.at[:, columns(g)], kv.at[OWN, g, i], local_sem.at[i, g])
            for i, hbm in ((0, k_hbm), (1, v_hbm))
        ]

    def flow(index, src_slot, dst_slot, target, g):
        return pltpu.make_async_remote_copy(
            src_ref=kv.at[src_slot, g],
            dst_ref=kv.at[dst_slot, g],
            send_sem=send_sem.at[index, g],
            recv_sem=recv_sem.at[dst_slot, g],
            device_id={"blk": target},
            device_id_type=pl.DeviceIdType.MESH,
        )

    def received(slot, sender, g):
        return pltpu.make_async_remote_copy(
            src_ref=kv.at[slot, g],
            dst_ref=kv.at[slot, g],
            send_sem=send_sem.at[0, g],
            recv_sem=recv_sem.at[slot, g],
            device_id={"blk": sender},
            device_id_type=pl.DeviceIdType.MESH,
        )

    own_flows = (
        (0, OWN, 5, d + 4, has_up),
        (1, OWN, 4, d - 4, has_down),
        (2, OWN, 3 - upper, pair, None),
        (3, OWN, 1 - odd, mate, None),
    )
    both = jnp.logical_and(has_up, has_down)
    pass_flows = (
        (4, 5, 7, d + 4, both),
        (5, 4, 6, d - 4, both),
        (6, 4 + upper, 2 + upper, pair, jnp.where(upper == 1, d - 4 >= 0, d + 4 < n)),
    )
    mate_flows = (
        (7, 2 + odd, odd, mate, jnp.where(odd == 1, d - 2 >= 0, d + 2 < n)),
    )

    def when(condition, action):
        if condition is None:
            action()
        else:
            pl.when(condition)(action)

    def start(flows, g):
        for index, src, dst, target, condition in flows:
            when(condition, lambda: flow(index, src, dst, target, g).start())

    def arrive(slot, sender, condition, g):
        when(condition, lambda: received(slot, sender, g).wait_recv())

    barrier = pltpu.get_barrier_semaphore()
    for target, condition in ((d + 4, has_up), (d - 4, has_down), (pair, None), (mate, None)):
        when(
            condition,
            lambda: pl.semaphore_signal(
                barrier, inc=1, device_id={"blk": target}, device_id_type=pl.DeviceIdType.MESH
            ),
        )

    @pl.loop(0, groups)
    def _(g):
        for c in local_copies(g):
            c.start()

    q_copy = pltpu.make_async_copy(q_hbm, q_vmem, q_sem)
    q_copy.start()
    kept_copy = pltpu.make_async_copy(kept_hbm, kept_ref, kept_sem)
    kept_copy.start()
    pl.semaphore_wait(barrier, 2 + has_up.astype(jnp.int32) + has_down.astype(jnp.int32))

    def send_own(g):
        for c in local_copies(g):
            c.wait()
        start(own_flows, g)

    for g in range(min(LEAD, groups)):
        send_own(g)

    for slot, offset in enumerate(OFFSETS[:OWN]):
        source = d + offset

        @pl.when(jnp.logical_or(source < 0, source >= n))
        def _():
            @pl.loop(0, groups)
            def _(g):
                kv[slot, g] = jnp.zeros(kv.shape[2:], kv.dtype)

    kept_copy.wait()
    for query_slot in range(local_blocks):
        kept = [kept_ref[query_slot, j] for j in range(kept_ref.shape[1])]
        for slot, offset in enumerate(OFFSETS):
            for key_slot in range(local_blocks):
                block = (d + offset) * local_blocks + key_slot
                allowed = functools.reduce(jnp.logical_or, [j == block for j in kept])
                allowed = jnp.logical_and(allowed, jnp.logical_and(d + offset >= 0, d + offset < n))
                bias[pl.ds(query_slot, 1), pl.ds(slot * rows + key_slot * BLOCK, BLOCK)] = jnp.full(
                    (1, BLOCK), jnp.where(allowed, 0.0, MASKED), jnp.float32
                )
    q_copy.wait()

    def out_copy(g):
        return pltpu.make_async_copy(
            out_ref.at[:, columns(g)], out_hbm.at[:, columns(g)], out_sem.at[g]
        )

    def attend(g):
        for head in range(width // DH):
            lanes = pl.ds(head * DH, DH)
            q = q_vmem[:, pl.ds(pl.multiple_of(g * width + head * DH, DH), DH)]
            tops = [None] * local_blocks
            for slot in range(len(OFFSETS)):
                s = lax.dot_general(
                    q, kv[slot, g, 0, :, lanes], (((1,), (1,)), ((), ())),
                    preferred_element_type=jnp.float32,
                )
                for b in range(local_blocks):
                    part = s[b * BLOCK : (b + 1) * BLOCK] + bias[b : b + 1, slot * rows : (slot + 1) * rows]
                    scores[slot, b * BLOCK : (b + 1) * BLOCK] = part
                    tops[b] = part if tops[b] is None else jnp.maximum(tops[b], part)
            top = jnp.concatenate([jnp.max(t, axis=1, keepdims=True) for t in tops], axis=0)
            sums = None
            numerator = None
            for slot in range(len(OFFSETS)):
                weight = jnp.exp2((scores[slot] - top) * C_EXP)
                sums = weight if sums is None else sums + weight
                term = jnp.dot(
                    weight.astype(jnp.bfloat16), kv[slot, g, 1, :, lanes],
                    preferred_element_type=jnp.float32,
                )
                numerator = term if numerator is None else numerator + term
            total = jnp.sum(sums, axis=1, keepdims=True)
            out_ref[:, pl.ds(pl.multiple_of(g * width + head * DH, DH), DH)] = (
                numerator / total
            ).astype(out_ref.dtype)
        out_copy(g).start()

    @pl.loop(0, groups + 2)
    def _(t):
        @pl.when(t + LEAD < groups)
        def _():
            send_own(t + LEAD)

        @pl.when(t < groups)
        def _():
            arrive(5, d - 4, has_down, t)
            arrive(4, d + 4, has_up, t)
            start(pass_flows, t)

        @pl.when(jnp.logical_and(t >= 1, t < groups + 1))
        def _():
            g = t - 1
            arrive(2 + upper, pair, None, g)
            arrive(3 - upper, pair, jnp.where(upper == 1, d + 2 < n, d - 2 >= 0), g)
            start(mate_flows, g)

        @pl.when(t >= 2)
        def _():
            g = t - 2
            arrive(odd, mate, None, g)
            arrive(1 - odd, mate, jnp.where(odd == 1, d + 1 < n, d - 1 >= 0), g)
            arrive(7, d - 4, d - 8 >= 0, g)
            arrive(6, d + 4, d + 8 < n, g)
            attend(g)

    @pl.loop(0, groups)
    def _(g):
        for index, src, dst, target, condition in own_flows + pass_flows + mate_flows:
            when(condition, lambda: flow(index, src, dst, target, g).wait_send())
        out_copy(g).wait()


def per_device(queries, keys, values, kept_blocks):
    n = lax.axis_size("blk")
    rows, features = queries.shape
    width = HEADS_PER_GROUP * DH
    groups = features // width
    slots = len(OFFSETS)
    return pl.pallas_call(
        functools.partial(kernel, n, groups),
        out_shape=jax.ShapeDtypeStruct((rows, features), jnp.bfloat16),
        in_specs=[pl.BlockSpec(memory_space=pltpu.HBM)] * 4,
        out_specs=pl.BlockSpec(memory_space=pltpu.HBM),
        scratch_shapes=[
            pltpu.VMEM((slots, groups, 2, rows, width), jnp.bfloat16),
            pltpu.SMEM(kept_blocks.shape, jnp.int32),
            pltpu.VMEM((rows, features), jnp.bfloat16),
            pltpu.VMEM((slots, rows, rows), jnp.float32),
            pltpu.VMEM((rows // BLOCK, slots * rows), jnp.float32),
            pltpu.VMEM((rows, features), jnp.bfloat16),
            pltpu.SemaphoreType.DMA((2, groups)),
            pltpu.SemaphoreType.DMA,
            pltpu.SemaphoreType.DMA,
            pltpu.SemaphoreType.DMA((groups,)),
            pltpu.SemaphoreType.DMA((8, groups)),
            pltpu.SemaphoreType.DMA((8, groups)),
        ],
        compiler_params=pltpu.CompilerParams(
            collective_id=0, has_side_effects=True, vmem_limit_bytes=67_043_328
        ),
    )(kept_blocks, queries, keys, values)


def solution(mesh):
    placed = P(("clip", "blk"), None)
    return jax.shard_map(
        per_device, mesh=mesh, in_specs=(placed,) * 4, out_specs=placed, check_vma=False
    )
```

```python
import functools
import math

import jax
import jax.numpy as jnp
from jax import lax
from jax.experimental import pallas as pl
from jax.experimental.pallas import tpu as pltpu
from jax.sharding import PartitionSpec as P

DH = 128
BLOCK = 128
SINGLES = 4
LEAD = 1

OFFSETS = (1, -1, 2, -2, 4, -4, 8, -8, 0)
OWN = 8
MASKED = -1e30
C_EXP = math.log2(math.e) / math.sqrt(DH)


def kernel(
    n, heads, doubles, kept_hbm, q_hbm, k_hbm, v_hbm, out_hbm,
    kv, kept_ref, q_vmem, scores, bias, out_vmem, local_sem, kept_sem, q_sem, out_sem, send_sem, recv_sem,
):
    groups = heads - doubles
    rows = kv.shape[-2]
    local_blocks = rows // BLOCK
    d = lax.axis_index("blk")
    r = lax.rem(d, 4)
    upper = r // 2
    odd = lax.rem(r, 2)

    pair = d + 2 - 4 * upper
    mate = d + 1 - 2 * odd
    has_up = d + 4 < n
    has_down = d - 4 >= 0

    def columns(h):
        return pl.ds(pl.multiple_of(h * DH, DH), DH)

    def by_size(g, action):
        @pl.when(g < doubles)
        def _():
            action(g * 2, 2)

        @pl.when(g >= doubles)
        def _():
            action(g + doubles, 1)

    def local_copies(h):
        return [
            pltpu.make_async_copy(hbm.at[:, columns(h)], kv.at[OWN, h, i], local_sem.at[i, h])
            for i, hbm in ((0, k_hbm), (1, v_hbm))
        ]

    def flow(index, src_slot, dst_slot, target, g, first, size):
        return pltpu.make_async_remote_copy(
            src_ref=kv.at[src_slot, pl.ds(first, size)],
            dst_ref=kv.at[dst_slot, pl.ds(first, size)],
            send_sem=send_sem.at[index, g],
            recv_sem=recv_sem.at[dst_slot, g],
            device_id={"blk": target},
            device_id_type=pl.DeviceIdType.MESH,
        )

    def received(slot, sender, g, first, size):
        return pltpu.make_async_remote_copy(
            src_ref=kv.at[slot, pl.ds(first, size)],
            dst_ref=kv.at[slot, pl.ds(first, size)],
            send_sem=send_sem.at[0, g],
            recv_sem=recv_sem.at[slot, g],
            device_id={"blk": sender},
            device_id_type=pl.DeviceIdType.MESH,
        )

    own_flows = (
        (0, OWN, 5, d + 4, has_up),
        (1, OWN, 4, d - 4, has_down),
        (2, OWN, 3 - upper, pair, None),
        (3, OWN, 1 - odd, mate, None),
    )
    both = jnp.logical_and(has_up, has_down)
    pass_flows = (
        (4, 5, 7, d + 4, both),
        (5, 4, 6, d - 4, both),
        (6, 4 + upper, 2 + upper, pair, jnp.where(upper == 1, d - 4 >= 0, d + 4 < n)),
    )
    mate_flows = (
        (7, 2 + odd, odd, mate, jnp.where(odd == 1, d - 2 >= 0, d + 2 < n)),
    )

    def when(condition, action):
        if condition is None:
            action()
        else:
            pl.when(condition)(action)

    def start(flows, *chunk):
        for index, src, dst, target, condition in flows:
            when(condition, lambda: flow(index, src, dst, target, *chunk).start())

    def arrive(slot, sender, condition, *chunk):
        when(condition, lambda: received(slot, sender, *chunk).wait_recv())

    barrier = pltpu.get_barrier_semaphore()
    for target, condition in ((d + 4, has_up), (d - 4, has_down), (pair, None), (mate, None)):
        when(
            condition,
            lambda: pl.semaphore_signal(
                barrier, inc=1, device_id={"blk": target}, device_id_type=pl.DeviceIdType.MESH
            ),
        )

    @pl.loop(0, heads)
    def _(h):
        for c in local_copies(h):
            c.start()

    q_copy = pltpu.make_async_copy(q_hbm, q_vmem, q_sem)
    q_copy.start()
    kept_copy = pltpu.make_async_copy(kept_hbm, kept_ref, kept_sem)
    kept_copy.start()
    pl.semaphore_wait(barrier, 2 + has_up.astype(jnp.int32) + has_down.astype(jnp.int32))

    def send_own(g):
        def action(first, size):
            for h in range(size):
                for c in local_copies(first + h):
                    c.wait()
            start(own_flows, g, first, size)

        by_size(g, action)

    def clear(first, size):
        for slot, offset in enumerate(OFFSETS[:OWN]):
            source = d + offset

            @pl.when(jnp.logical_or(source < 0, source >= n))
            def _():
                for h in range(size):
                    kv[slot, first + h] = jnp.zeros(kv.shape[2:], kv.dtype)

    def prepare():
        kept_copy.wait()
        for query_slot in range(local_blocks):
            kept = [kept_ref[query_slot, j] for j in range(kept_ref.shape[1])]
            for slot, offset in enumerate(OFFSETS):
                inside = jnp.logical_and(d + offset >= 0, d + offset < n)
                for key_slot in range(local_blocks):
                    block = (d + offset) * local_blocks + key_slot
                    allowed = functools.reduce(jnp.logical_or, [j == block for j in kept])
                    bias[pl.ds(query_slot, 1), pl.ds(slot * rows + key_slot * BLOCK, BLOCK)] = jnp.full(
                        (1, BLOCK), jnp.where(jnp.logical_and(allowed, inside), 0.0, MASKED), jnp.float32
                    )
        q_copy.wait()

    for g in range(min(LEAD, groups)):
        send_own(jnp.int32(g))

    def out_copy(h):
        return pltpu.make_async_copy(
            out_vmem.at[:, columns(h)], out_hbm.at[:, columns(h)], out_sem.at[h]
        )

    def attend(h, arrivals):
        q = q_vmem[:, columns(h)]
        tops = [None] * local_blocks
        for step, slot in enumerate((8, 2, 3, 4, 5, 0, 1, 6, 7)):
            if step == 5:
                arrivals()
            s = lax.dot_general(
                q, kv[slot, h, 0], (((1,), (1,)), ((), ())), preferred_element_type=jnp.float32
            )
            for b in range(local_blocks):
                part = s[b * BLOCK : (b + 1) * BLOCK] + bias[b : b + 1, slot * rows : (slot + 1) * rows]
                scores[slot, b * BLOCK : (b + 1) * BLOCK] = part
                tops[b] = part if tops[b] is None else jnp.maximum(tops[b], part)
        top = jnp.concatenate([jnp.max(t, axis=1, keepdims=True) for t in tops], axis=0)
        sums = None
        numerator = None
        for slot in range(len(OFFSETS)):
            weight = jnp.exp2((scores[slot] - top) * C_EXP)
            sums = weight if sums is None else sums + weight
            term = jnp.dot(
                weight.astype(jnp.bfloat16), kv[slot, h, 1], preferred_element_type=jnp.float32
            )
            numerator = term if numerator is None else numerator + term
        total = jnp.sum(sums, axis=1, keepdims=True)
        out_vmem[:, columns(h)] = numerator / total
        out_copy(h).start()

    @pl.loop(0, groups + 2)
    def _(t):
        @pl.when(t + LEAD < groups)
        def _():
            send_own(t + LEAD)

        @pl.when(t < groups)
        def _():
            def action(first, size):
                clear(first, size)
                arrive(5, d - 4, has_down, t, first, size)
                arrive(4, d + 4, has_up, t, first, size)
                start(pass_flows, t, first, size)

            by_size(t, action)

        @pl.when(t == 0)
        def _():
            prepare()

        @pl.when(jnp.logical_and(t >= 1, t < groups + 1))
        def _():
            g = t - 1

            def action(*chunk):
                arrive(2 + upper, pair, None, g, *chunk)
                arrive(3 - upper, pair, jnp.where(upper == 1, d + 2 < n, d - 2 >= 0), g, *chunk)
                start(mate_flows, g, *chunk)

            by_size(g, action)

        @pl.when(t >= 2)
        def _():
            g = t - 2

            def action(first, size):
                def arrivals():
                    arrive(odd, mate, None, g, first, size)
                    arrive(1 - odd, mate, jnp.where(odd == 1, d + 1 < n, d - 1 >= 0), g, first, size)
                    arrive(7, d - 4, d - 8 >= 0, g, first, size)
                    arrive(6, d + 4, d + 8 < n, g, first, size)

                for h in range(size):
                    attend(first + h, arrivals if h == 0 else lambda: None)

            by_size(g, action)

    @pl.loop(0, groups)
    def _(g):
        def action(first, size):
            for index, src, dst, target, condition in own_flows + pass_flows + mate_flows:
                when(condition, lambda: flow(index, src, dst, target, g, first, size).wait_send())
            for h in range(size):
                out_copy(first + h).wait()

        by_size(g, action)


def per_device(queries, keys, values, kept_blocks):
    n = lax.axis_size("blk")
    rows, features = queries.shape
    heads = features // DH
    doubles = max(heads - SINGLES, 0) // 2
    groups = heads - doubles
    slots = len(OFFSETS)
    attended = pl.pallas_call(
        functools.partial(kernel, n, heads, doubles),
        out_shape=jax.ShapeDtypeStruct((rows, features), jnp.float32),
        in_specs=[pl.BlockSpec(memory_space=pltpu.HBM)] * 4,
        out_specs=pl.BlockSpec(memory_space=pltpu.HBM),
        scratch_shapes=[
            pltpu.VMEM((slots, heads, 2, rows, DH), jnp.bfloat16),
            pltpu.SMEM(kept_blocks.shape, jnp.int32),
            pltpu.VMEM((rows, features), jnp.bfloat16),
            pltpu.VMEM((slots, rows, rows), jnp.float32),
            pltpu.VMEM((rows // BLOCK, slots * rows), jnp.float32),
            pltpu.VMEM((rows, features), jnp.float32),
            pltpu.SemaphoreType.DMA((2, heads)),
            pltpu.SemaphoreType.DMA,
            pltpu.SemaphoreType.DMA,
            pltpu.SemaphoreType.DMA((heads,)),
            pltpu.SemaphoreType.DMA((8, groups)),
            pltpu.SemaphoreType.DMA((8, groups)),
        ],
        compiler_params=pltpu.CompilerParams(
            collective_id=0, has_side_effects=True, vmem_limit_bytes=67_043_328
        ),
    )(kept_blocks, queries, keys, values)
    return attended.astype(jnp.bfloat16)


def solution(mesh):
    placed = P(("clip", "blk"), None)
    return jax.shard_map(
        per_device, mesh=mesh, in_specs=(placed,) * 4, out_specs=placed, check_vma=False
    )
```
